32 devices in a mesh: dp: 8 (over z, x), tensor: 4 (over y, core).
Axes of the slice: x: 2, y: 2, z: 4, core: 2. Of those that a mesh axis runs over, the one named last changes fastest.
Arguments:
- images: bfloat16 [16, 197, 768], P('dp'), may hold values from -6 to 6
- image_counts: int32 [8], P('dp'), may hold values from 1 to 2, as said below
- first_norm_gain: float32 [768], replicated, may hold values from 0.5 to 1.5
- first_norm_bias: float32 [768], replicated, may hold values from -3 to 3
- qkv_weight: bfloat16 [768, 3, 768], P(None, None, 'tensor'), may hold values from -2 to 2
- qv_bias: float32 [2, 768], P(None, 'tensor'), may hold values from -3 to 3
- out_weight: bfloat16 [768, 768], P('tensor'), may hold values from -1.25 to 1.25
- out_bias: float32 [768], replicated, may hold values from -3 to 3
- second_norm_gain: float32 [768], replicated, may hold values from 0.5 to 1.5
- second_norm_bias: float32 [768], replicated, may hold values from -3 to 3
- fc1_weight: bfloat16 [768, 3072], P(None, 'tensor'), may hold values from -0.21875 to 0.21875
- fc1_bias: float32 [3072], P('tensor'), may hold values from -3 to 3
- fc2_weight: bfloat16 [3072, 768], P('tensor'), may hold values from -0.15625 to 0.15625
- fc2_bias: float32 [768], replicated, may hold values from -3 to 3
- cotangent: bfloat16 [16, 197, 768], P('dp'), may hold values from -6 to 6
Outputs:
- block_out: bfloat16 [16, 197, 768], P('dp')
- input_grad: bfloat16 [16, 197, 768], P('dp')
- grad_first_norm_gain: float32 [768], replicated
- grad_first_norm_bias: float32 [768], replicated
- grad_qkv_weight: float32 [768, 3, 768], P(None, None, 'tensor')
- grad_qv_bias: float32 [2, 768], P(None, 'tensor')
- grad_out_weight: float32 [768, 768], P('tensor')
- grad_out_bias: float32 [768], replicated
- grad_second_norm_gain: float32 [768], replicated
- grad_second_norm_bias: float32 [768], replicated
- grad_fc1_weight: float32 [768, 3072], P(None, 'tensor')
- grad_fc1_bias: float32 [3072], P('tensor')
- grad_fc2_weight: float32 [3072, 768], P('tensor')
- grad_fc2_bias: float32 [768], replicated
The draws below stay inside these ranges and needn't reach their ends.
Inputs may be any that keep to these rules, and one draw needn't show every extreme that they name: `image_counts`: some index of dp has 2 live slots and some has 1; live slots come first in each index's block of 2.
All inputs are finite; a program needn't handle non-finite values.
Results may differ from the reference program's by a relative error of at most 0.02.
Values may be sent and summed in bfloat16 or wider, within the bound.
A program may use at most 128 MiB of HBM per device.

```python
import jax
import jax.numpy as jnp
from jax import lax

D = 768
HEADS = 12
HEAD_DIM = 64
MLP = 3072
SEQ = 197
IMG_CAP = 2
IMAGES = 16
N_DP = 8
N_TENSOR = 4


def draw_image_counts(key, part):
    key_counts, key_full, key_lone = jax.random.split(key, 3)
    counts = jax.random.randint(key_counts, (N_DP,), 1, IMG_CAP + 1)
    full_slot = jax.random.randint(key_full, (), 0, N_DP)
    lone_slot = (full_slot + 1 + jax.random.randint(key_lone, (), 0, N_DP - 1)) % N_DP
    counts = counts.at[full_slot].set(IMG_CAP)
    counts = counts.at[lone_slot].set(1)
    return counts.astype(jnp.int32)


def draw_qkv_weight(key, part):
    key_base = jax.random.fold_in(key, 0)
    normal_part = jax.random.truncated_normal(key_base, -6.0, 6.0, (D, 3, D), jnp.float32) * D ** (-0.5)
    return normal_part.astype(jnp.bfloat16)


def level_of(rng, shape, cuts, least, high):
    gain, own = 1.0, jax.random.fold_in(rng, 6)
    for position, blocks in cuts:
        steps = jnp.exp(jax.random.uniform(jax.random.fold_in(own, position), (blocks,), jnp.float32, least / len(cuts), high / len(cuts)))
        gain = gain * jnp.repeat(steps, shape[position] // blocks).reshape([-1 if axis == position else 1 for axis in range(len(shape))])
    return gain


def bell_draw(stream_key, shape, spread, reach, shards=(), kind=jnp.bfloat16):
    array = jax.random.normal(stream_key, shape, jnp.float32) * spread
    if len(shards) > 0:
        array = level_of(stream_key, shape, shards, -0.22, 0.18) * array
    return jnp.clip(array, min=-reach, max=reach).astype(kind)


def setup_inputs(seed: int = 0) -> dict:
    streams_of = jax.random.split(jax.random.key(seed), 16)
    return {
        "images": bell_draw(streams_of[0], (IMAGES, SEQ, D), 1.0, 6.0, ((0, 8),)),
        "image_counts": draw_image_counts(jax.random.fold_in(streams_of[15], 71), 0),
        "first_norm_gain": jnp.clip(1.0 + 0.1 * jax.random.normal(streams_of[2], (D,), jnp.float32), 0.5, 1.5),
        "first_norm_bias": bell_draw(streams_of[3], (D,), 0.5, 3.0, (), jnp.float32),
        "qkv_weight": draw_qkv_weight(jax.random.fold_in(streams_of[15], 71), 0),
        "qv_bias": bell_draw(streams_of[5], (2, D), 0.5, 3.0, ((1, 4),), jnp.float32),
        "out_weight": bell_draw(streams_of[6], (D, D), (D // 32) ** -0.5, 1.25, ((0, 4),)),
        "out_bias": bell_draw(streams_of[7], (D,), 0.5, 3.0, (), jnp.float32),
        "second_norm_gain": jnp.clip(1.0 + 0.1 * jax.random.normal(streams_of[8], (D,), jnp.float32), 0.5, 1.5),
        "second_norm_bias": bell_draw(streams_of[9], (D,), 0.5, 3.0, (), jnp.float32),
        "fc1_weight": bell_draw(streams_of[10], (D, MLP), D ** -0.5, 0.21875, ((1, 4),)),
        "fc1_bias": bell_draw(streams_of[11], (MLP,), 0.5, 3.0, ((0, 4),), jnp.float32),
        "fc2_weight": bell_draw(streams_of[12], (MLP, D), (MLP // 2) ** -0.5, 0.15625, ((0, 4),)),
        "fc2_bias": bell_draw(streams_of[13], (D,), 0.5, 3.0, (), jnp.float32),
        "cotangent": bell_draw(streams_of[14], (IMAGES, SEQ, D), 1.0, 6.0, ((0, 8),)),
    }


EPS = 1e-06
ROOT_HALF = 0.7071067811865476
INV_ROOT_TAU = 0.3989422804014327

def to_half(array_in):
    return array_in.astype(jnp.bfloat16)

def rounded(array_in):
    return lax.optimization_barrier(array_in.astype(jnp.bfloat16)).astype(jnp.float32)

def norm_forward(row_values, gain_vec, shift_vec):
    centre = row_values - lax.optimization_barrier(jnp.mean(row_values, axis=-1, keepdims=True))
    inverse = lax.rsqrt(lax.optimization_barrier(jnp.mean(centre * centre, axis=-1, keepdims=True)) + EPS)
    scaled = centre * inverse
    return (scaled * gain_vec + shift_vec, scaled, inverse)

def norm_backward(grad_out, scaled, inverse, gain_vec):
    grad_scaled = grad_out * gain_vec
    grad_rows = inverse * (grad_scaled - lax.optimization_barrier(jnp.mean(grad_scaled, axis=-1, keepdims=True)) - scaled * lax.optimization_barrier(jnp.mean(grad_scaled * scaled, axis=-1, keepdims=True)))
    return (grad_rows, lax.optimization_barrier(jnp.sum(grad_out * scaled, axis=0)), lax.optimization_barrier(jnp.sum(grad_out, axis=0)))

def gelu_value(pre_act):
    return 0.5 * pre_act * (1.0 + jax.scipy.special.erf(pre_act * ROOT_HALF))

def gelu_slope(pre_act):
    return 0.5 * (1.0 + jax.scipy.special.erf(pre_act * ROOT_HALF)) + pre_act * jnp.exp(-0.5 * pre_act * pre_act) * INV_ROOT_TAU

def reference(images, image_counts, first_norm_gain, first_norm_bias, qkv_weight, qv_bias, out_weight, out_bias, second_norm_gain, second_norm_bias, fc1_weight, fc1_bias, fc2_weight, fc2_bias, cotangent):
    f32 = jnp.float32
    group_width = D // N_TENSOR
    hidden_group = MLP // N_TENSOR
    score_scale = HEAD_DIM ** (-0.5)
    slot_index = jnp.arange(IMAGES, dtype=jnp.int32)
    live_slots = (slot_index % IMG_CAP < image_counts[slot_index // IMG_CAP]).astype(f32)
    qkv_flat = qkv_weight.reshape(D, 3 * D)
    qkv_groups = qkv_weight.astype(f32).reshape(D, 3, N_TENSOR, group_width)
    out_groups = out_weight.astype(f32).reshape(N_TENSOR, group_width, D)
    fc1_groups = fc1_weight.astype(f32).reshape(D, N_TENSOR, hidden_group)
    fc2_groups = fc2_weight.astype(f32).reshape(N_TENSOR, hidden_group, D)
    qkv_shift = jnp.stack([qv_bias[0], jnp.zeros((D,), f32), qv_bias[1]])

    def image_step(totals, image_item):
        image_rows, image_cot, live_flag = image_item
        row_values = image_rows.astype(f32)
        norm_one, scaled_one, inverse_one = norm_forward(row_values, first_norm_gain, first_norm_bias)
        norm_one = to_half(norm_one)
        qkv_rows = to_half(jnp.dot(norm_one, qkv_flat, preferred_element_type=f32).reshape(SEQ, 3, D) + qkv_shift)
        queries = qkv_rows[:, 0].reshape(SEQ, HEADS, HEAD_DIM)
        key_heads = qkv_rows[:, 1].reshape(SEQ, HEADS, HEAD_DIM)
        value_heads = qkv_rows[:, 2].reshape(SEQ, HEADS, HEAD_DIM)
        scores = jnp.einsum('qhd,khd->hqk', queries.astype(f32), key_heads.astype(f32)) * score_scale
        row_peak = lax.optimization_barrier(jnp.max(scores, axis=-1, keepdims=True))
        log_total = row_peak + jnp.log(lax.optimization_barrier(jnp.sum(jnp.exp(scores - row_peak), axis=-1, keepdims=True)))
        probs_full = jnp.exp(scores - log_total)
        probs_half = to_half(probs_full)
        context = to_half(jnp.einsum('hqk,khd->qhd', probs_half.astype(f32), value_heads.astype(f32))).reshape(SEQ, D)
        attn_parts = jnp.einsum('sgk,gkd->gsd', context.astype(f32).reshape(SEQ, N_TENSOR, group_width), out_groups)
        resid_rows = row_values + lax.optimization_barrier(jnp.sum(rounded(attn_parts), axis=0)) + out_bias
        norm_two, scaled_two, inverse_two = norm_forward(resid_rows, second_norm_gain, second_norm_bias)
        norm_two = to_half(norm_two)
        pre_act = jnp.dot(norm_two, fc1_weight, preferred_element_type=f32) + fc1_bias
        act_half = to_half(gelu_value(pre_act))
        mlp_parts = jnp.einsum('sgm,gmd->gsd', act_half.astype(f32).reshape(SEQ, N_TENSOR, hidden_group), fc2_groups)
        final_rows = resid_rows + lax.optimization_barrier(jnp.sum(rounded(mlp_parts), axis=0)) + fc2_bias
        block_rows = to_half(final_rows * live_flag)
        grad_final = image_cot.astype(f32) * live_flag
        grad_final_half = to_half(grad_final)
        grad_act = jnp.dot(grad_final_half, fc2_weight.T, preferred_element_type=f32)
        grad_pre = grad_act * gelu_slope(pre_act)
        grad_pre_half = to_half(grad_pre)
        two_parts = jnp.einsum('sgm,dgm->gsd', grad_pre_half.astype(f32).reshape(SEQ, N_TENSOR, hidden_group), fc1_groups)
        grad_norm_two = lax.optimization_barrier(jnp.sum(rounded(two_parts), axis=0))
        back_two, gain_two, shift_two = norm_backward(grad_norm_two, scaled_two, inverse_two, second_norm_gain)
        grad_resid = grad_final + back_two
        grad_resid_half = to_half(grad_resid)
        grad_context = to_half(jnp.dot(grad_resid_half, out_weight.T, preferred_element_type=f32)).reshape(SEQ, HEADS, HEAD_DIM)
        grad_probs = jnp.einsum('qhd,khd->hqk', grad_context.astype(f32), value_heads.astype(f32))
        grad_scores = to_half(probs_full * (grad_probs - lax.optimization_barrier(jnp.sum(probs_full * grad_probs, axis=-1, keepdims=True))) * score_scale)
        grad_queries = jnp.einsum('hqk,khd->qhd', grad_scores.astype(f32), key_heads.astype(f32)).reshape(SEQ, D)
        grad_keys = jnp.einsum('hqk,qhd->khd', grad_scores.astype(f32), queries.astype(f32)).reshape(SEQ, D)
        grad_values = jnp.einsum('hqk,qhd->khd', probs_half.astype(f32), grad_context.astype(f32)).reshape(SEQ, D)
        grad_qkv = jnp.stack([grad_queries, grad_keys, grad_values], axis=1)
        grad_qkv_half = to_half(grad_qkv)
        one_parts = jnp.einsum('scgk,dcgk->gsd', grad_qkv_half.astype(f32).reshape(SEQ, 3, N_TENSOR, group_width), qkv_groups)
        grad_norm_one = lax.optimization_barrier(jnp.sum(rounded(one_parts), axis=0))
        back_one, gain_one, shift_one = norm_backward(grad_norm_one, scaled_one, inverse_one, first_norm_gain)
        input_rows = to_half(grad_resid + back_one)
        grad_terms = (gain_one, shift_one, jnp.dot(norm_one.T, grad_qkv_half.reshape(SEQ, 3 * D), preferred_element_type=f32), jnp.stack([lax.optimization_barrier(jnp.sum(grad_queries, axis=0)), lax.optimization_barrier(jnp.sum(grad_values, axis=0))]), jnp.dot(context.T, grad_resid_half, preferred_element_type=f32), lax.optimization_barrier(jnp.sum(grad_resid, axis=0)), gain_two, shift_two, jnp.dot(norm_two.T, grad_pre_half, preferred_element_type=f32), lax.optimization_barrier(jnp.sum(grad_pre, axis=0)), jnp.dot(act_half.T, grad_final_half, preferred_element_type=f32), lax.optimization_barrier(jnp.sum(grad_final, axis=0)))
        return (jax.tree.map(jnp.add, totals, grad_terms), (block_rows, input_rows))
    start = (jnp.zeros((D,), f32), jnp.zeros((D,), f32), jnp.zeros((D, 3 * D), f32), jnp.zeros((2, D), f32), jnp.zeros((D, D), f32), jnp.zeros((D,), f32), jnp.zeros((D,), f32), jnp.zeros((D,), f32), jnp.zeros((D, MLP), f32), jnp.zeros((MLP,), f32), jnp.zeros((MLP, D), f32), jnp.zeros((D,), f32))
    totals, stacked = lax.scan(image_step, start, (images, cotangent, live_slots))
    block_out, input_grad = stacked
    grads = [entry / IMAGES for entry in totals]
    return (block_out, input_grad, grads[0], grads[1], grads[2].reshape(D, 3, D), grads[3], grads[4], grads[5], grads[6], grads[7], grads[8], grads[9], grads[10], grads[11])
```

```python
import jax
import jax.numpy as jnp
from jax import lax
from jax.experimental import pallas as pl
from jax.experimental.pallas import tpu as pltpu
from jax.sharding import PartitionSpec as P

HEAD_DIM = 64


EPS = 1e-06
ROOT_HALF = 0.7071067811865476
INV_ROOT_TAU = 0.3989422804014327


def to_half(array_in):
    return array_in.astype(jnp.bfloat16)


def norm_forward(row_values, gain_vec, shift_vec):
    centre = row_values - jnp.mean(row_values, axis=-1, keepdims=True)
    inverse = lax.rsqrt(jnp.mean(centre * centre, axis=-1, keepdims=True) + EPS)
    scaled = centre * inverse
    return (scaled * gain_vec + shift_vec, scaled, inverse)


def norm_backward(grad_out, scaled, inverse, gain_vec):
    grad_scaled = grad_out * gain_vec
    grad_rows = inverse * (
        grad_scaled
        - jnp.mean(grad_scaled, axis=-1, keepdims=True)
        - scaled * jnp.mean(grad_scaled * scaled, axis=-1, keepdims=True)
    )
    return (grad_rows, jnp.sum(grad_out * scaled, axis=0), jnp.sum(grad_out, axis=0))


def gelu_value(pre_act):
    return 0.5 * pre_act * (1.0 + jax.scipy.special.erf(pre_act * ROOT_HALF))


def gelu_slope(pre_act):
    return (
        0.5 * (1.0 + jax.scipy.special.erf(pre_act * ROOT_HALF))
        + pre_act * jnp.exp(-0.5 * pre_act * pre_act) * INV_ROOT_TAU
    )


MESH = pl.DeviceIdType.MESH
ROW_TILE = 16


def log2_of(count):
    steps = count.bit_length() - 1
    assert 1 << steps == count
    return steps


def bit_of(axis, position):
    index = lax.axis_index(axis)
    bit = (index // (1 << position)) % 2
    return bit, index + (1 - 2 * bit) * (1 << position)


def greet(peers):
    barrier = pltpu.get_barrier_semaphore()
    for axis, position in peers:
        _, partner = bit_of(axis, position)
        pl.semaphore_signal(barrier, inc=1, device_id={axis: partner}, device_id_type=MESH)
    pl.semaphore_wait(barrier, len(peers))


class Wires:
    def __init__(self, send_sems, recv_sems):
        self.send_sems, self.recv_sems, self.copies = send_sems, recv_sems, []

    def start(self, source, target, axis, position):
        _, partner = bit_of(axis, position)
        slot = len(self.copies)
        copy = pltpu.make_async_remote_copy(
            src_ref=source,
            dst_ref=target,
            send_sem=self.send_sems.at[slot],
            recv_sem=self.recv_sems.at[slot],
            device_id={axis: partner},
            device_id_type=MESH,
        )
        copy.start()
        self.copies.append(copy)
        return copy

    def finish(self):
        for copy in self.copies:
            copy.wait_send()


def run_wavefront(streams):
    order = sorted(
        ((place + stage, -stage, place) for place, stages in enumerate(streams) for stage in range(len(stages)))
    )
    for _, minus_stage, place in order:
        streams[place][-minus_stage]()


def grad_stages(wires, axis, order, source, landing, result):
    steps = len(order)
    count = 1 << steps
    bits = [bit_of(axis, position)[0] for position in order]
    held = {}

    def start_halving(step):
        half = count >> (step + 1)
        block = source if step == 0 else landing[step - 1]
        held["copy"] = wires.start(
            block.at[pl.ds((1 - bits[step]) * half, half)], landing[step], axis, order[step]
        )

    def start_doubling(step):
        base = sum(bits[i] * (count >> (i + 1)) for i in range(step + 1))
        part = result.at[pl.ds(base, count >> (step + 1))]
        held["copy"] = wires.start(part, part, axis, order[step])

    def add_stage(step):
        def stage():
            held["copy"].wait_recv()
            half = count >> (step + 1)
            block = source if step == 0 else landing[step - 1]
            if step < steps - 1:
                @pl.loop(0, half)
                def _(i):
                    mine = block[bits[step] * half + i].astype(jnp.float32)
                    theirs = landing[step][i].astype(jnp.float32)
                    landing[step][i] = (mine + theirs).astype(jnp.bfloat16)

                start_halving(step + 1)
            else:
                base = sum(bits[i] * (count >> (i + 1)) for i in range(steps))
                mine = block[bits[step]].astype(jnp.float32)
                theirs = landing[step][0].astype(jnp.float32)
                result[base] = (mine + theirs).astype(jnp.bfloat16)
                start_doubling(steps - 1)

        return stage

    def gather_stage(step):
        def stage():
            held["copy"].wait_recv()
            if step > 0:
                start_doubling(step - 1)

        return stage

    return (
        [lambda: start_halving(0)]
        + [add_stage(step) for step in range(steps)]
        + [gather_stage(step) for step in reversed(range(steps))]
    )


def vector_stages(wires, axis, steps, source, landing, sums, result):
    held = {}

    def current(step):
        return source if step == 0 else sums.at[step - 1]

    def start(step):
        held["copy"] = wires.start(current(step), landing.at[step], axis, step)

    def stage_of(step):
        def stage():
            held["copy"].wait_recv()
            total = current(step)[...] + landing[step]
            if step < steps - 1:
                sums[step] = total
                start(step + 1)
            else:
                result[...] = total

        return stage

    return [lambda: start(0)] + [stage_of(step) for step in range(steps)]


def share_stages(wires, axis, steps, source, landing, sums, result, columns):
    near = bit_of(axis, 0)[0]
    held = {}

    def start(step):
        if step == 0:
            held["copy"] = wires.start(
                source.at[1 - near, :, columns], landing.at[0, :, columns], axis, 0
            )
        else:
            held["copy"] = wires.start(
                sums.at[step - 1, :, columns], landing.at[step, :, columns], axis, step
            )

    def stage_of(step):
        def stage():
            held["copy"].wait_recv()
            mine = source[near, :, columns] if step == 0 else sums[step - 1, :, columns]
            total = mine.astype(jnp.float32) + landing[step, :, columns].astype(jnp.float32)
            total = total.astype(jnp.bfloat16)
            if step < steps - 1:
                sums[step, :, columns] = total
                start(step + 1)
            else:
                result[near, :, columns] = total
                part = result.at[near, :, columns]
                held["copy"] = wires.start(part, part, axis, 0)

        return stage

    return (
        [lambda: start(0)]
        + [stage_of(step) for step in range(steps)]
        + [lambda: held["copy"].wait_recv()]
    )


def column_cuts(width, pieces):
    size = width // pieces
    if width % pieces or size % 128:
        return [slice(0, width)]
    return [slice(i * size, (i + 1) * size) for i in range(pieces)]


VMEM_SPEC = pl.BlockSpec(memory_space=pltpu.VMEM)


def tensor_sum(part):
    rows, width = part.shape
    steps = log2_of(lax.axis_size("tensor"))
    cuts = column_cuts(width, 3)

    def kernel(part_ref, out_ref, landing, sums, send_sems, recv_sems):
        greet([("tensor", position) for position in range(steps)])
        wires = Wires(send_sems, recv_sems)
        run_wavefront(
            [share_stages(wires, "tensor", steps, part_ref, landing, sums, out_ref, cut) for cut in cuts]
        )
        wires.finish()

    copies = len(cuts) * (steps + 1)
    return pl.pallas_call(
        kernel,
        out_shape=jax.ShapeDtypeStruct((2, rows // 2, width), jnp.bfloat16),
        in_specs=[VMEM_SPEC],
        out_specs=VMEM_SPEC,
        scratch_shapes=[
            pltpu.VMEM((steps, rows // 2, width), jnp.bfloat16),
            pltpu.VMEM((steps, rows // 2, width), jnp.bfloat16),
            pltpu.SemaphoreType.DMA((copies,)),
            pltpu.SemaphoreType.DMA((copies,)),
        ],
        compiler_params=pltpu.CompilerParams(collective_id=0, has_side_effects=True),
        name="tensor_sum",
    )(part.reshape(2, rows // 2, width)).reshape(rows, width)


def grad_sum(grads, vectors, part):
    count = lax.axis_size("dp")
    steps = log2_of(count)
    tensor_steps = log2_of(lax.axis_size("tensor"))
    rows, width = part.shape
    cuts = column_cuts(width, 3)
    blocks = []
    for grad in grads:
        pieces = 3 if grad.shape[0] % (3 * count * ROW_TILE) == 0 else 1
        blocks.append(grad.reshape(pieces, count, grad.shape[0] // (pieces * count), grad.shape[1]))
    total = len(blocks)
    far_first = [*range(1, steps), 0]
    near_first = [*range(steps)]

    def kernel(*refs):
        sources, (vector_ref, part_ref) = refs[:total], refs[total : total + 2]
        results, (vector_out, part_out) = refs[total + 2 : 2 * total + 2], refs[2 * total + 2 : 2 * total + 4]
        scratch = refs[2 * total + 4 :]
        landings = [scratch[i * steps : (i + 1) * steps] for i in range(total)]
        vector_landing, vector_sums, part_landing, part_sums, send_sems, recv_sems = scratch[total * steps :]
        greet(
            [("dp", position) for position in range(steps)]
            + [("tensor", position) for position in range(tensor_steps)]
        )
        wires = Wires(send_sems, recv_sems)
        streams = [vector_stages(wires, "dp", steps, vector_ref, vector_landing, vector_sums, vector_out)]
        for which in range(total):
            pieces = blocks[which].shape[0]
            for piece in range(pieces):
                order = far_first if which < 2 and piece == 0 else near_first
                streams.append(
                    grad_stages(
                        wires,
                        "dp",
                        order,
                        sources[which].at[piece],
                        [landing.at[piece] for landing in landings[which]],
                        results[which].at[piece],
                    )
                )
        for place, cut in enumerate(cuts):
            streams.insert(
                1 + place,
                share_stages(wires, "tensor", tensor_steps, part_ref, part_landing, part_sums, part_out, cut),
            )
        run_wavefront(streams)
        wires.finish()

    copies = steps + sum(block.shape[0] for block in blocks) * 2 * steps + len(cuts) * (tensor_steps + 1)
    scratch_shapes = []
    for block in blocks:
        for step in range(steps):
            scratch_shapes.append(
                pltpu.VMEM((block.shape[0], count >> (step + 1), *block.shape[2:]), jnp.bfloat16)
            )
    scratch_shapes += [
        pltpu.VMEM((steps, *vectors.shape), jnp.float32),
        pltpu.VMEM((steps, *vectors.shape), jnp.float32),
        pltpu.VMEM((tensor_steps, rows // 2, width), jnp.bfloat16),
        pltpu.VMEM((tensor_steps, rows // 2, width), jnp.bfloat16),
        pltpu.SemaphoreType.DMA((copies,)),
        pltpu.SemaphoreType.DMA((copies,)),
    ]
    outs = pl.pallas_call(
        kernel,
        out_shape=[jax.ShapeDtypeStruct(block.shape, jnp.bfloat16) for block in blocks]
        + [
            jax.ShapeDtypeStruct(vectors.shape, jnp.float32),
            jax.ShapeDtypeStruct((2, rows // 2, width), jnp.bfloat16),
        ],
        in_specs=[VMEM_SPEC] * (total + 2),
        out_specs=[VMEM_SPEC] * (total + 2),
        scratch_shapes=scratch_shapes,
        compiler_params=pltpu.CompilerParams(collective_id=1, has_side_effects=True),
        name="grad_sum",
    )(*blocks, vectors, part.reshape(2, rows // 2, width))
    summed = [out.reshape(grad.shape).astype(jnp.float32) for out, grad in zip(outs, grads)]
    return summed, outs[total], outs[total + 1].reshape(rows, width)


def per_device(
    images,
    image_counts,
    first_norm_gain,
    first_norm_bias,
    qkv_weight,
    qv_bias,
    out_weight,
    out_bias,
    second_norm_gain,
    second_norm_bias,
    fc1_weight,
    fc1_bias,
    fc2_weight,
    fc2_bias,
    cotangent,
):
    f32 = jnp.float32
    slot_count, true_length, model_width = images.shape
    length = -(-true_length // ROW_TILE) * ROW_TILE
    token_pad = ((0, 0), (0, length - true_length), (0, 0))
    images = jnp.pad(images, token_pad)
    cotangent = jnp.pad(cotangent, token_pad)
    key_live = jnp.arange(length) < true_length
    local_width = qkv_weight.shape[2]
    local_heads = local_width // HEAD_DIM
    row_count = slot_count * length
    score_scale = HEAD_DIM ** (-0.5)
    live_slots = (jnp.arange(slot_count, dtype=jnp.int32) < image_counts[0]).astype(f32)
    row_live = jnp.broadcast_to(live_slots[:, None], (slot_count, length)).reshape(row_count, 1)
    head_shape = (slot_count, length, local_heads, HEAD_DIM)
    row_values = images.reshape(row_count, model_width).astype(f32)
    norm_one, scaled_one, inverse_one = norm_forward(row_values, first_norm_gain, first_norm_bias)
    norm_one = to_half(norm_one)
    qkv_flat = qkv_weight.reshape(model_width, 3 * local_width)
    qkv_shift = jnp.stack([qv_bias[0], jnp.zeros_like(qv_bias[0]), qv_bias[1]])
    qkv_rows = to_half(
        jnp.dot(norm_one, qkv_flat, preferred_element_type=f32).reshape(row_count, 3, local_width)
        + qkv_shift
    )
    queries = qkv_rows[:, 0].reshape(head_shape)
    key_heads = qkv_rows[:, 1].reshape(head_shape)
    value_heads = qkv_rows[:, 2].reshape(head_shape)
    scores = (
        jnp.einsum("bqhd,bkhd->bhqk", queries, key_heads, preferred_element_type=f32) * score_scale
    )
    scores = jnp.where(key_live, scores, -jnp.inf)
    row_peak = jnp.max(scores, axis=-1, keepdims=True)
    log_total = row_peak + jnp.log(jnp.sum(jnp.exp(scores - row_peak), axis=-1, keepdims=True))
    probs_full = jnp.exp(scores - log_total)
    probs_half = to_half(probs_full)
    context = to_half(
        jnp.einsum("bhqk,bkhd->bqhd", probs_half, value_heads, preferred_element_type=f32)
    )
    context_rows = context.reshape(row_count, local_width)
    attn_part = jnp.dot(context_rows, out_weight, preferred_element_type=f32)
    resid_rows = (
        row_values
        + tensor_sum(attn_part.astype(jnp.bfloat16)).astype(jnp.float32)
        + out_bias
    )
    norm_two, scaled_two, inverse_two = norm_forward(resid_rows, second_norm_gain, second_norm_bias)
    norm_two = to_half(norm_two)
    pre_act = jnp.dot(norm_two, fc1_weight, preferred_element_type=f32) + fc1_bias
    act_half = to_half(gelu_value(pre_act))
    mlp_part = jnp.dot(act_half, fc2_weight, preferred_element_type=f32)
    inv_images = 1.0 / (slot_count * lax.axis_size("dp"))
    grad_final = cotangent.reshape(row_count, model_width).astype(f32) * row_live
    grad_final_half = to_half(grad_final)
    grad_act = jnp.dot(grad_final_half, fc2_weight.T, preferred_element_type=f32)
    grad_pre = grad_act * gelu_slope(pre_act)
    grad_pre_half = to_half(grad_pre)
    two_part = jnp.dot(grad_pre_half, fc1_weight.T, preferred_element_type=f32)
    grad_norm_two = tensor_sum(two_part.astype(jnp.bfloat16)).astype(jnp.float32)
    back_two, gain_two, shift_two = norm_backward(
        grad_norm_two, scaled_two, inverse_two, second_norm_gain
    )
    grad_resid = grad_final + back_two
    grad_resid_half = to_half(grad_resid)
    grad_context = to_half(
        jnp.dot(grad_resid_half, out_weight.T, preferred_element_type=f32)
    ).reshape(head_shape)
    grad_probs = jnp.einsum(
        "bqhd,bkhd->bhqk", grad_context, value_heads, preferred_element_type=f32
    )
    grad_scores = to_half(
        probs_full
        * (grad_probs - jnp.sum(probs_full * grad_probs, axis=-1, keepdims=True))
        * score_scale
    )
    grad_queries = jnp.einsum(
        "bhqk,bkhd->bqhd", grad_scores, key_heads, preferred_element_type=f32
    ).reshape(row_count, local_width)
    grad_keys = jnp.einsum(
        "bhqk,bqhd->bkhd", grad_scores, queries, preferred_element_type=f32
    ).reshape(row_count, local_width)
    grad_values = jnp.einsum(
        "bhqk,bqhd->bkhd", probs_half, grad_context, preferred_element_type=f32
    ).reshape(row_count, local_width)
    grad_qkv_half = to_half(jnp.stack([grad_queries, grad_keys, grad_values], axis=1)).reshape(
        row_count, 3 * local_width
    )
    one_part = jnp.dot(grad_qkv_half, qkv_flat.T, preferred_element_type=f32)
    grad_norm_one = tensor_sum(one_part.astype(jnp.bfloat16)).astype(jnp.float32)
    back_one, gain_one, shift_one = norm_backward(
        grad_norm_one, scaled_one, inverse_one, first_norm_gain
    )
    input_grad = to_half(grad_resid + back_one).reshape(slot_count, length, model_width)[:, :true_length]
    weight_grads = [
        to_half(jnp.dot(left.T, right, preferred_element_type=f32) * inv_images)
        for left, right in (
            (norm_two, grad_pre_half),
            (act_half, grad_final_half),
            (norm_one, grad_qkv_half),
            (context_rows, grad_resid_half),
        )
    ]
    rows = [
        gain_one,
        shift_one,
        jnp.sum(grad_resid, axis=0),
        gain_two,
        shift_two,
        jnp.sum(grad_final, axis=0),
        jnp.sum(grad_pre, axis=0),
        jnp.sum(grad_queries, axis=0),
        jnp.sum(grad_values, axis=0),
    ]
    vector_width = -(-max(row.shape[0] for row in rows) // 128) * 128
    vectors = jnp.stack([jnp.pad(row, (0, vector_width - row.shape[0])) for row in rows])
    vectors = jnp.pad(vectors * inv_images, ((0, -len(rows) % 8), (0, 0)))
    (fc1_grad, fc2_grad, qkv_grad, out_grad), vectors, mlp_sum = grad_sum(
        weight_grads, vectors, to_half(mlp_part)
    )
    final_rows = resid_rows + mlp_sum.astype(f32) + fc2_bias
    block_out = to_half(final_rows * row_live).reshape(slot_count, length, model_width)[:, :true_length]
    return (
        block_out,
        input_grad,
        vectors[0, :model_width],
        vectors[1, :model_width],
        qkv_grad.reshape(model_width, 3, local_width),
        vectors[7:9, :local_width],
        out_grad,
        vectors[2, :model_width],
        vectors[3, :model_width],
        vectors[4, :model_width],
        fc1_grad,
        vectors[6, : fc1_bias.shape[0]],
        fc2_grad,
        vectors[5, :model_width],
    )


def solution(mesh):
    placed = (
        P("dp", None, None),
        P("dp"),
        P(),
        P(),
        P(None, None, "tensor"),
        P(None, "tensor"),
        P("tensor", None),
        P(),
        P(),
        P(),
        P(None, "tensor"),
        P("tensor"),
        P("tensor", None),
        P(),
        P("dp", None, None),
    )
    return jax.shard_map(
        per_device,
        mesh=mesh,
        in_specs=placed,
        out_specs=(
            P("dp", None, None),
            P("dp", None, None),
            P(),
            P(),
            P(None, None, "tensor"),
            P(None, "tensor"),
            P("tensor", None),
            P(),
            P(),
            P(),
            P(None, "tensor"),
            P("tensor"),
            P("tensor", None),
            P(),
        ),
        check_vma=False,
    )
```

```python
import jax
import jax.numpy as jnp
from jax import lax
from jax.experimental import pallas as pl
from jax.experimental.pallas import tpu as pltpu
from jax.sharding import PartitionSpec as P

HEAD_DIM = 64


EPS = 1e-06
ROOT_HALF = 0.7071067811865476
INV_ROOT_TAU = 0.3989422804014327


def to_half(array_in):
    return array_in.astype(jnp.bfloat16)


def norm_forward(row_values, gain_vec, shift_vec):
    centre = row_values - jnp.mean(row_values, axis=-1, keepdims=True)
    inverse = lax.rsqrt(jnp.mean(centre * centre, axis=-1, keepdims=True) + EPS)
    scaled = centre * inverse
    return (scaled * gain_vec + shift_vec, scaled, inverse)


def norm_backward(grad_out, scaled, inverse, gain_vec):
    grad_scaled = grad_out * gain_vec
    grad_rows = inverse * (
        grad_scaled
        - jnp.mean(grad_scaled, axis=-1, keepdims=True)
        - scaled * jnp.mean(grad_scaled * scaled, axis=-1, keepdims=True)
    )
    return (grad_rows, jnp.sum(grad_out * scaled, axis=0), jnp.sum(grad_out, axis=0))


def gelu_value(pre_act):
    return 0.5 * pre_act * (1.0 + jax.scipy.special.erf(pre_act * ROOT_HALF))


def gelu_slope(pre_act):
    return (
        0.5 * (1.0 + jax.scipy.special.erf(pre_act * ROOT_HALF))
        + pre_act * jnp.exp(-0.5 * pre_act * pre_act) * INV_ROOT_TAU
    )


MESH = pl.DeviceIdType.MESH
ROW_TILE = 16


def log2_of(count):
    steps = count.bit_length() - 1
    assert 1 << steps == count
    return steps


def bit_of(axis, position):
    index = lax.axis_index(axis)
    bit = (index // (1 << position)) % 2
    return bit, index + (1 - 2 * bit) * (1 << position)


def greet(peers):
    barrier = pltpu.get_barrier_semaphore()
    for axis, position in peers:
        _, partner = bit_of(axis, position)
        pl.semaphore_signal(barrier, inc=1, device_id={axis: partner}, device_id_type=MESH)
    pl.semaphore_wait(barrier, len(peers))


class Wires:
    def __init__(self, send_sems, recv_sems):
        self.send_sems, self.recv_sems, self.copies = send_sems, recv_sems, []

    def start(self, source, target, axis, position):
        _, partner = bit_of(axis, position)
        slot = len(self.copies)
        copy = pltpu.make_async_remote_copy(
            src_ref=source,
            dst_ref=target,
            send_sem=self.send_sems.at[slot],
            recv_sem=self.recv_sems.at[slot],
            device_id={axis: partner},
            device_id_type=MESH,
        )
        copy.start()
        self.copies.append(copy)
        return copy

    def finish(self):
        for copy in self.copies:
            copy.wait_send()


def run_wavefront(streams):
    order = sorted(
        ((place + stage, -stage, place) for place, stages in enumerate(streams) for stage in range(len(stages)))
    )
    for _, minus_stage, place in order:
        streams[place][-minus_stage]()


def grad_stages(wires, axis, order, source, landing, result):
    steps = len(order)
    count = 1 << steps
    bits = [bit_of(axis, position)[0] for position in order]
    held = {}

    def start_halving(step):
        half = count >> (step + 1)
        block = source if step == 0 else landing[step - 1]
        held["copy"] = wires.start(
            block.at[pl.ds((1 - bits[step]) * half, half)], landing[step], axis, order[step]
        )

    def start_doubling(step):
        base = sum(bits[i] * (count >> (i + 1)) for i in range(step + 1))
        part = result.at[pl.ds(base, count >> (step + 1))]
        held["copy"] = wires.start(part, part, axis, order[step])

    def add_stage(step):
        def stage():
            held["copy"].wait_recv()
            half = count >> (step + 1)
            block = source if step == 0 else landing[step - 1]
            if step < steps - 1:
                @pl.loop(0, half)
                def _(i):
                    mine = block[bits[step] * half + i].astype(jnp.float32)
                    theirs = landing[step][i].astype(jnp.float32)
                    landing[step][i] = (mine + theirs).astype(jnp.bfloat16)

                start_halving(step + 1)
            else:
                base = sum(bits[i] * (count >> (i + 1)) for i in range(steps))
                mine = block[bits[step]].astype(jnp.float32)
                theirs = landing[step][0].astype(jnp.float32)
                result[base] = (mine + theirs).astype(jnp.bfloat16)
                start_doubling(steps - 1)

        return stage

    def gather_stage(step):
        def stage():
            held["copy"].wait_recv()
            if step > 0:
                start_doubling(step - 1)

        return stage

    return (
        [lambda: start_halving(0)]
        + [add_stage(step) for step in range(steps)]
        + [gather_stage(step) for step in reversed(range(steps))]
    )


def vector_stages(wires, axis, steps, source, landing, sums, result):
    held = {}

    def current(step):
        return source if step == 0 else sums.at[step - 1]

    def start(step):
        held["copy"] = wires.start(current(step), landing.at[step], axis, step)

    def stage_of(step):
        def stage():
            held["copy"].wait_recv()
            total = current(step)[...] + landing[step]
            if step < steps - 1:
                sums[step] = total
                start(step + 1)
            else:
                result[...] = total

        return stage

    return [lambda: start(0)] + [stage_of(step) for step in range(steps)]


def share_stages(wires, axis, steps, source, landing, sums, result, columns):
    near = bit_of(axis, 0)[0]
    held = {}

    def start(step):
        if step == 0:
            held["copy"] = wires.start(
                source.at[1 - near, :, columns], landing.at[0, :, columns], axis, 0
            )
        else:
            held["copy"] = wires.start(
                sums.at[step - 1, :, columns], landing.at[step, :, columns], axis, step
            )

    def stage_of(step):
        def stage():
            held["copy"].wait_recv()
            mine = source[near, :, columns] if step == 0 else sums[step - 1, :, columns]
            total = mine.astype(jnp.float32) + landing[step, :, columns].astype(jnp.float32)
            total = total.astype(jnp.bfloat16)
            if step < steps - 1:
                sums[step, :, columns] = total
                start(step + 1)
            else:
                result[near, :, columns] = total
                part = result.at[near, :, columns]
                held["copy"] = wires.start(part, part, axis, 0)

        return stage

    return (
        [lambda: start(0)]
        + [stage_of(step) for step in range(steps)]
        + [lambda: held["copy"].wait_recv()]
    )


def column_cuts(width, pieces):
    size = width // pieces
    if width % pieces or size % 128:
        return [slice(0, width)]
    return [slice(i * size, (i + 1) * size) for i in range(pieces)]


VMEM_SPEC = pl.BlockSpec(memory_space=pltpu.VMEM)


def tensor_sum(part):
    rows, width = part.shape
    steps = log2_of(lax.axis_size("tensor"))
    cuts = column_cuts(width, 3)

    def kernel(part_ref, out_ref, landing, sums, send_sems, recv_sems):
        greet([("tensor", position) for position in range(steps)])
        wires = Wires(send_sems, recv_sems)
        run_wavefront(
            [share_stages(wires, "tensor", steps, part_ref, landing, sums, out_ref, cut) for cut in cuts]
        )
        wires.finish()

    copies = len(cuts) * (steps + 1)
    return pl.pallas_call(
        kernel,
        out_shape=jax.ShapeDtypeStruct((2, rows // 2, width), jnp.bfloat16),
        in_specs=[VMEM_SPEC],
        out_specs=VMEM_SPEC,
        scratch_shapes=[
            pltpu.VMEM((steps, rows // 2, width), jnp.bfloat16),
            pltpu.VMEM((steps, rows // 2, width), jnp.bfloat16),
            pltpu.SemaphoreType.DMA((copies,)),
            pltpu.SemaphoreType.DMA((copies,)),
        ],
        compiler_params=pltpu.CompilerParams(collective_id=0, has_side_effects=True),
        name="tensor_sum",
    )(part.reshape(2, rows // 2, width)).reshape(rows, width)


def dot_nt(left, right):
    return lax.dot_general(left, right, (((1,), (1,)), ((), ())), preferred_element_type=jnp.float32)


def dot_tn(left, right):
    return lax.dot_general(left, right, (((0,), (0,)), ((), ())), preferred_element_type=jnp.float32)


def dot_nn(left, right):
    return jnp.dot(left, right, preferred_element_type=jnp.float32)


def backward_tail(
    fc1_grad,
    fc2_grad,
    mlp_part,
    two_part,
    scaled_two,
    inverse_two,
    second_gain,
    grad_final_half,
    out_weight,
    queries_t,
    keys_t,
    value_heads,
    probs,
    norm_one,
    context_t,
    qkv_weight_t,
    scaled_one,
    inverse_one,
    first_gain,
    vectors,
):
    f32 = jnp.float32
    count = lax.axis_size("dp")
    steps = log2_of(count)
    tensor_steps = log2_of(lax.axis_size("tensor"))
    slots, length, width = two_part.shape
    local_width = out_weight.shape[0]
    heads = local_width // HEAD_DIM
    cuts = column_cuts(width, 3)
    inv_images = 1.0 / (slots * count)
    score_scale = HEAD_DIM ** (-0.5)
    share_rows = local_width // count
    early = []
    for grad in (fc1_grad, fc2_grad):
        pieces = 3 if grad.shape[0] % (3 * count * ROW_TILE) == 0 else 1
        early.append(grad.reshape(pieces, count, grad.shape[0] // (pieces * count), grad.shape[1]))
    late_shape = (4, count, share_rows, width)
    far_first = [*range(1, steps), 0]
    near_first = [*range(steps)]

    def kernel(
        fc1_ref, fc2_ref, mlp_ref, two_ref, scaled_two_ref, inverse_two_ref, second_gain_ref,
        final_ref, out_weight_ref, queries_ref, keys_ref, values_ref, probs_ref, norm_ref,
        context_ref, qkv_weight_ref, scaled_one_ref, inverse_one_ref, first_gain_ref, vector_in_ref,
        fc1_out, fc2_out, late_out, vector_out, mlp_out, input_out,
        two_sum, one_ref, one_sum, resid, resid_half, late, vector_ref, qkv_t,
        vector_landing, vector_sums, share_landing, share_sums, send_sems, recv_sems, *landings,
    ):
        greet(
            [("tensor", position) for position in range(tensor_steps)]
            + [("dp", position) for position in range(steps)]
        )
        wires = Wires(send_sems, recv_sems)
        agenda = []

        def plan(time, action):
            agenda.append((time, len(agenda), action))

        def plan_all(actions, begin, gap, first=None):
            for place, action in enumerate(actions):
                plan(begin + gap * place if place or first is None else first, action)

        def shares(which, source, result, begin):
            for place, cut in enumerate(cuts):
                stages = share_stages(
                    wires, "tensor", tensor_steps, source,
                    share_landing.at[which], share_sums.at[which], result, cut,
                )
                plan(begin, stages[0])
                for stage, action in enumerate(stages[1:]):
                    plan(begin + 2 + 3.5 * stage + 3 * place, action)

        vector_ref[...] = vector_in_ref[...]

        def resid_stage(slot):
            def stage():
                grad = two_sum[slot].astype(f32)
                scaled = scaled_two_ref[slot]
                back, gain, shift = norm_backward(grad, scaled, inverse_two_ref[slot], second_gain_ref[...])
                total = final_ref[slot].astype(f32) + back
                resid[slot] = total
                resid_half[slot] = to_half(total)
                for row, value in ((2, jnp.sum(total, axis=0)), (3, gain), (4, shift)):
                    vector_ref[row : row + 1, :width] += value[None] * inv_images

            return stage

        def head_stage(slot, head):
            def stage():
                at = slot * heads + head
                weight = out_weight_ref[head * HEAD_DIM : (head + 1) * HEAD_DIM]
                grad_context = to_half(dot_nt(resid_half[slot], weight))
                grad_context_t = to_half(dot_nt(weight, resid_half[slot]))
                grad_probs = dot_nt(grad_context, values_ref[at])
                full = probs_ref[at]
                inner = jnp.sum(full * grad_probs, axis=-1, keepdims=True)
                grad_scores = to_half(full * (grad_probs - inner) * score_scale)
                terms = (
                    dot_nt(keys_ref[at], grad_scores),
                    dot_nn(queries_ref[at], grad_scores),
                    dot_nn(grad_context_t, to_half(full)),
                )
                ones = jnp.ones((8, length), f32)
                for part, term in enumerate(terms):
                    begin = part * local_width + head * HEAD_DIM
                    qkv_t[slot, begin : begin + HEAD_DIM, :] = to_half(term)
                    if part != 1:
                        sums = lax.dot_general(
                            ones, term, (((1,), (1,)), ((), ())),
                            precision=lax.Precision.HIGHEST, preferred_element_type=f32,
                        )
                        row = 7 + (part // 2) * heads + head
                        vector_ref[row : row + 1, :HEAD_DIM] += sums[0:1] * inv_images

            return stage

        def late_stage(part):
            def stage():
                total = jnp.zeros((local_width, width), f32)
                for slot in range(slots):
                    if part < 3:
                        left = qkv_t[slot, part * local_width : (part + 1) * local_width, :]
                        total += dot_nn(left, norm_ref[slot])
                    else:
                        total += dot_nn(context_ref[slot], resid_half[slot])
                total = total * inv_images
                for block in range(count):
                    late[part, block] = to_half(total[block * share_rows : (block + 1) * share_rows])

            return stage

        def one_stage(slot):
            def stage():
                one_ref[slot] = to_half(dot_tn(qkv_t[slot], qkv_weight_ref[...]))

            return stage

        def input_stage(slot):
            def stage():
                grad = one_sum[slot].astype(f32)
                back, gain, shift = norm_backward(
                    grad, scaled_one_ref[slot], inverse_one_ref[slot], first_gain_ref[...]
                )
                input_out[slot] = to_half(resid[slot] + back)
                for row, value in ((0, gain), (1, shift)):
                    vector_ref[row : row + 1, :width] += value[None] * inv_images

            return stage

        shares(0, two_ref, two_sum, -2)
        streams = 0
        for which, (source, result) in enumerate(((fc1_ref, fc1_out), (fc2_ref, fc2_out))):
            for piece in range(early[which].shape[0]):
                stages = grad_stages(
                    wires, "dp", far_first if piece == 0 else near_first, source.at[piece],
                    [landings[which * steps + step].at[piece] for step in range(steps)], result.at[piece],
                )
                plan_all(stages, 4 + 6 * streams, 7, 0.5)
                streams += 1
        for slot in range(slots):
            plan(14, resid_stage(slot))
        for slot in range(slots):
            for head in range(heads):
                plan(15 + 1.5 * (slot * heads + head), head_stage(slot, head))
        for slot in range(slots):
            plan(25, one_stage(slot))
        shares(1, one_ref, one_sum, 26)
        for part in range(4):
            plan(27 + part, late_stage(part))
            stages = grad_stages(
                wires, "dp", near_first, late.at[part],
                [landings[2 * steps + step].at[part] for step in range(steps)], late_out.at[part],
            )
            plan_all(stages, max(4 + 6 * streams, 24 + part), 7, 27 + part)
            streams += 1
        for slot in range(slots):
            plan(42, input_stage(slot))
        plan_all(
            vector_stages(wires, "dp", steps, vector_ref, vector_landing, vector_sums, vector_out), 43, 16
        )
        shares(2, mlp_ref, mlp_out, 44)
        for _, _, action in sorted(agenda, key=lambda entry: entry[:2]):
            action()
        wires.finish()

    copies = steps + (sum(block.shape[0] for block in early) + 4) * 2 * steps + 3 * len(cuts) * (tensor_steps + 1)
    scratch_shapes = [
        pltpu.VMEM(two_part.shape, jnp.bfloat16),
        pltpu.VMEM(two_part.shape, jnp.bfloat16),
        pltpu.VMEM(two_part.shape, jnp.bfloat16),
        pltpu.VMEM(two_part.shape, f32),
        pltpu.VMEM(two_part.shape, jnp.bfloat16),
        pltpu.VMEM(late_shape, jnp.bfloat16),
        pltpu.VMEM(vectors.shape, f32),
        pltpu.VMEM((slots, 3 * local_width, length), jnp.bfloat16),
        pltpu.VMEM((steps, *vectors.shape), f32),
        pltpu.VMEM((steps, *vectors.shape), f32),
        pltpu.VMEM((3, tensor_steps, length, width), jnp.bfloat16),
        pltpu.VMEM((3, tensor_steps, length, width), jnp.bfloat16),
        pltpu.SemaphoreType.DMA((copies,)),
        pltpu.SemaphoreType.DMA((copies,)),
    ]
    for shape in (early[0].shape, early[1].shape, late_shape):
        for step in range(steps):
            scratch_shapes.append(pltpu.VMEM((shape[0], count >> (step + 1), *shape[2:]), jnp.bfloat16))
    fc1_sum, fc2_sum, late_sum, vectors, mlp_sum, input_grad = pl.pallas_call(
        kernel,
        out_shape=[
            jax.ShapeDtypeStruct(early[0].shape, jnp.bfloat16),
            jax.ShapeDtypeStruct(early[1].shape, jnp.bfloat16),
            jax.ShapeDtypeStruct(late_shape, jnp.bfloat16),
            jax.ShapeDtypeStruct(vectors.shape, f32),
            jax.ShapeDtypeStruct(mlp_part.shape, jnp.bfloat16),
            jax.ShapeDtypeStruct(two_part.shape, jnp.bfloat16),
        ],
        in_specs=[VMEM_SPEC] * 20,
        out_specs=[VMEM_SPEC] * 6,
        scratch_shapes=scratch_shapes,
        compiler_params=pltpu.CompilerParams(collective_id=1, has_side_effects=True),
        name="backward_tail",
    )(
        *early, mlp_part, two_part, scaled_two, inverse_two, second_gain, grad_final_half, out_weight,
        queries_t, keys_t, value_heads, probs, norm_one, context_t, qkv_weight_t, scaled_one,
        inverse_one, first_gain, vectors,
    )
    late_sum = late_sum.reshape(4, local_width, width)
    return (
        fc1_sum.reshape(fc1_grad.shape).astype(f32),
        fc2_sum.reshape(fc2_grad.shape).astype(f32),
        jnp.transpose(late_sum[:3], (2, 0, 1)).astype(f32),
        late_sum[3].astype(f32),
        vectors,
        mlp_sum,
        input_grad,
    )


def per_device(
    images,
    image_counts,
    first_norm_gain,
    first_norm_bias,
    qkv_weight,
    qv_bias,
    out_weight,
    out_bias,
    second_norm_gain,
    second_norm_bias,
    fc1_weight,
    fc1_bias,
    fc2_weight,
    fc2_bias,
    cotangent,
):
    f32 = jnp.float32
    slot_count, true_length, model_width = images.shape
    length = -(-true_length // ROW_TILE) * ROW_TILE
    token_pad = ((0, 0), (0, length - true_length), (0, 0))
    images = jnp.pad(images, token_pad)
    cotangent = jnp.pad(cotangent, token_pad)
    key_live = jnp.arange(length) < true_length
    local_width = qkv_weight.shape[2]
    local_heads = local_width // HEAD_DIM
    row_count = slot_count * length
    score_scale = HEAD_DIM ** (-0.5)
    live_slots = (jnp.arange(slot_count, dtype=jnp.int32) < image_counts[0]).astype(f32)
    row_live = jnp.broadcast_to(live_slots[:, None], (slot_count, length)).reshape(row_count, 1)
    head_shape = (slot_count, length, local_heads, HEAD_DIM)
    row_values = images.reshape(row_count, model_width).astype(f32)
    norm_one, scaled_one, inverse_one = norm_forward(row_values, first_norm_gain, first_norm_bias)
    norm_one = to_half(norm_one)
    qkv_flat = qkv_weight.reshape(model_width, 3 * local_width)
    qkv_shift = jnp.stack([qv_bias[0], jnp.zeros_like(qv_bias[0]), qv_bias[1]])
    qkv_rows = to_half(
        jnp.dot(norm_one, qkv_flat, preferred_element_type=f32).reshape(row_count, 3, local_width)
        + qkv_shift
    )
    queries = qkv_rows[:, 0].reshape(head_shape)
    key_heads = qkv_rows[:, 1].reshape(head_shape)
    value_heads = qkv_rows[:, 2].reshape(head_shape)
    scores = (
        jnp.einsum("bqhd,bkhd->bhqk", queries, key_heads, preferred_element_type=f32) * score_scale
    )
    scores = jnp.where(key_live, scores, -jnp.inf)
    row_peak = jnp.max(scores, axis=-1, keepdims=True)
    log_total = row_peak + jnp.log(jnp.sum(jnp.exp(scores - row_peak), axis=-1, keepdims=True))
    probs_full = jnp.exp(scores - log_total)
    probs_half = to_half(probs_full)
    context = to_half(
        jnp.einsum("bhqk,bkhd->bqhd", probs_half, value_heads, preferred_element_type=f32)
    )
    context_rows = context.reshape(row_count, local_width)
    context_t = jnp.transpose(context, (0, 2, 3, 1)).reshape(slot_count, local_width, length)
    attn_part = jnp.dot(context_rows, out_weight, preferred_element_type=f32)
    resid_rows = (
        row_values
        + tensor_sum(attn_part.astype(jnp.bfloat16)).astype(jnp.float32)
        + out_bias
    )
    norm_two, scaled_two, inverse_two = norm_forward(resid_rows, second_norm_gain, second_norm_bias)
    norm_two = to_half(norm_two)
    pre_act = jnp.dot(norm_two, fc1_weight, preferred_element_type=f32) + fc1_bias
    act_half = to_half(gelu_value(pre_act))
    mlp_part = jnp.dot(act_half, fc2_weight, preferred_element_type=f32)
    inv_images = 1.0 / (slot_count * lax.axis_size("dp"))
    grad_final = cotangent.reshape(row_count, model_width).astype(f32) * row_live
    grad_final_half = to_half(grad_final)
    grad_act = jnp.dot(grad_final_half, fc2_weight.T, preferred_element_type=f32)
    grad_pre = grad_act * gelu_slope(pre_act)
    grad_pre_half = to_half(grad_pre)
    two_part = jnp.dot(grad_pre_half, fc1_weight.T, preferred_element_type=f32)
    per_slot = (slot_count, length, model_width)
    per_head = slot_count * local_heads
    rows = [jnp.sum(grad_final, axis=0) * inv_images, jnp.sum(grad_pre, axis=0) * inv_images]
    vector_width = -(-max(model_width, fc1_bias.shape[0]) // 128) * 128
    vector_rows = -(-(7 + 2 * local_heads) // 8) * 8
    vectors = jnp.stack([jnp.pad(row, (0, vector_width - row.shape[0])) for row in rows])
    vectors = jnp.pad(vectors, ((5, vector_rows - 7), (0, 0)))
    fc1_grad = to_half(jnp.dot(norm_two.T, grad_pre_half, preferred_element_type=f32) * inv_images)
    fc2_grad = to_half(jnp.dot(act_half.T, grad_final_half, preferred_element_type=f32) * inv_images)
    fc1_grad, fc2_grad, qkv_grad, out_grad, vectors, mlp_sum, input_grad = backward_tail(
        fc1_grad,
        fc2_grad,
        to_half(mlp_part).reshape(per_slot),
        to_half(two_part).reshape(per_slot),
        scaled_two.reshape(per_slot),
        inverse_two.reshape(slot_count, length, 1),
        second_norm_gain[None],
        grad_final_half.reshape(per_slot),
        out_weight,
        jnp.transpose(queries, (0, 2, 3, 1)).reshape(per_head, HEAD_DIM, length),
        jnp.transpose(key_heads, (0, 2, 3, 1)).reshape(per_head, HEAD_DIM, length),
        jnp.transpose(value_heads, (0, 2, 1, 3)).reshape(per_head, length, HEAD_DIM),
        probs_full.reshape(per_head, length, length),
        norm_one.reshape(per_slot),
        context_t,
        qkv_flat.T,
        scaled_one.reshape(per_slot),
        inverse_one.reshape(slot_count, length, 1),
        first_norm_gain[None],
        vectors,
    )
    final_rows = resid_rows + mlp_sum.reshape(row_count, model_width).astype(f32) + fc2_bias
    block_out = to_half(final_rows * row_live).reshape(per_slot)[:, :true_length]
    input_grad = input_grad[:, :true_length]
    qv_grad = vectors[7 : 7 + 2 * local_heads, :HEAD_DIM].reshape(2, local_width)
    return (
        block_out,
        input_grad,
        vectors[0, :model_width],
        vectors[1, :model_width],
        qkv_grad,
        qv_grad,
        out_grad,
        vectors[2, :model_width],
        vectors[3, :model_width],
        vectors[4, :model_width],
        fc1_grad,
        vectors[6, : fc1_bias.shape[0]],
        fc2_grad,
        vectors[5, :model_width],
    )


def solution(mesh):
    placed = (
        P("dp", None, None),
        P("dp"),
        P(),
        P(),
        P(None, None, "tensor"),
        P(None, "tensor"),
        P("tensor", None),
        P(),
        P(),
        P(),
        P(None, "tensor"),
        P("tensor"),
        P("tensor", None),
        P(),
        P("dp", None, None),
    )
    return jax.shard_map(
        per_device,
        mesh=mesh,
        in_specs=placed,
        out_specs=(
            P("dp", None, None),
            P("dp", None, None),
            P(),
            P(),
            P(None, None, "tensor"),
            P(None, "tensor"),
            P("tensor", None),
            P(),
            P(),
            P(),
            P(None, "tensor"),
            P("tensor"),
            P("tensor", None),
            P(),
        ),
        check_vma=False,
    )
```
